32 devices in a mesh: ctx: 16 (over z, x, core), head: 2 (over y).
Axes of the slice: x: 2, y: 2, z: 4, core: 2. Of those that a mesh axis runs over, the one named last changes fastest.
Arguments:
- q_latent: bfloat16 [2048, 1536], P(('ctx', 'head')), may hold values from -320 to 320
- q_gain: float32 [1536], replicated, may hold values from 0.5 to 8
- kv_cache: bfloat16 [2048, 576], P(('ctx', 'head')), may hold values from -320 to 320
- kv_gain: float32 [512], replicated, may hold values from 0.5 to 8
- w_query: bfloat16 [1536, 12288], P(None, 'head'), may hold values from -0.15625 to 0.15625
- w_kv: bfloat16 [512, 16384], P(None, 'head'), may hold values from -0.25 to 0.25
- doc_lengths: int32 [3], replicated, may hold values from 1 to 1024, 2048 in all
Outputs:
- attn_out: bfloat16 [2048, 8192], P('ctx', 'head')
The draws below stay inside these ranges and needn't reach their ends.
Inputs may be any that keep to these rules, and one draw needn't show every extreme that they name: `doc_lengths`: 3 documents, lengths in order summing to 2048; the longest has exactly 1024 tokens.
All inputs are finite; a program needn't handle non-finite values.
Results may differ from the reference program's by a relative error of at most 0.0075.
The reference program's roundings to bfloat16 on the way count: a program that leaves them out, or rounds other values in their place, can miss the bound.
Values may be sent and summed in bfloat16 or wider, within the bound.
A program may use at most 192 MiB of HBM per device.

```python
import math
import jax
import jax.numpy as jnp
import numpy as np
from jax import lax

QL = 1536
KL = 512
RD = 64
ND = 128
VD = 128
HEADS = 64
DOCS = 3
SEQ = 2048


def scaled_rows(key, row_count, col_count, plain_cols):
    normal_key = jax.random.fold_in(key, 101)
    row_key = jax.random.fold_in(key, 202)
    col_key = jax.random.fold_in(key, 303)
    values = jax.random.truncated_normal(normal_key, -4.0, 4.0, (row_count, col_count), jnp.float32)
    row_top = math.log(10.0)
    row_scale = jnp.exp(jax.random.uniform(row_key, (row_count, 1), jnp.float32, 0.0, row_top))
    col_scale = jnp.exp(jax.random.uniform(col_key, (1, col_count), jnp.float32, 0.0, math.log(3.0)))
    column_index = jnp.arange(col_count, dtype=jnp.int32)[None, :]
    scaled = values * row_scale * col_scale
    return jnp.where(column_index < col_count - plain_cols, scaled, values)


def gain_values(key, width):
    return jax.random.uniform(key, (width,), jnp.float32, 0.5, 1.5)


def draw_q_latent(key, part):
    return scaled_rows(jax.random.fold_in(key, 11), SEQ, QL, 0).astype(jnp.bfloat16)


def draw_kv_cache(key, part):
    return scaled_rows(jax.random.fold_in(key, 23), SEQ, KL + RD, RD).astype(jnp.bfloat16)


def draw_q_gain(key, part):
    return gain_values(jax.random.fold_in(key, 37), QL)


def draw_kv_gain(key, part):
    return gain_values(jax.random.fold_in(key, 41), KL)


def block_levels(own_key, dims, pieces, smallest, high):
    factor_of = 1.0
    for axis_at, shards_of in pieces:
        draws = jax.random.uniform(jax.random.fold_in(jax.random.fold_in(own_key, 6), axis_at), (shards_of,), jnp.float32, smallest / len(pieces), high / len(pieces))
        factor_of = factor_of * jnp.repeat(jnp.exp(draws), dims[axis_at] // shards_of).reshape((-1,) + (1,) * (len(dims) - 1 - axis_at))
    return factor_of


def split_up(count, total, most, slope):
    loads = [(1 << 20) // math.isqrt(grade ** slope) + 1 for grade in range(2, count + 1)]
    surplus, holding = total - most - (count - 1), [1] * (count - 1)
    while surplus > 0:
        movable = [i for i in range(count - 1) if holding[i] < most]
        whole, budget = sum([loads[i] for i in movable]), surplus
        for i in movable:
            more = min(most - holding[i], max(1, budget * loads[i] // whole), surplus)
            holding[i] = holding[i] + more
            surplus = surplus - more
    return np.array([most] + holding)


def ragged(own_key, count, total, reach, slope):
    if count == 2:
        one = jax.random.randint(own_key, (), max(1, total - reach), min(reach, total - 1) + 1)
        return jnp.stack([one, total - one])
    sizes = jnp.asarray(split_up(count, total, reach, slope), jnp.int32)
    pairs = (count - 1) // 2
    source_of, receiver = sizes[1:1 + 2 * pairs:2], sizes[2:2 + 2 * pairs:2]
    slack = jnp.minimum(source_of - 1, reach - receiver)
    moved = jax.random.randint(jax.random.fold_in(own_key, 1), (pairs,), 0, 1 << 20) % (slack + 1)
    sizes = sizes.at[1:1 + 2 * pairs:2].set(source_of - moved).at[2:2 + 2 * pairs:2].set(receiver + moved)
    return sizes[jax.random.permutation(jax.random.fold_in(own_key, 2), count)]


def normal_values(own_key, dims, scale, reach, pieces=(), kind=jnp.bfloat16):
    level = block_levels(own_key, dims, pieces, -0.22, 0.18) if pieces else 1.0
    entries = jax.random.normal(own_key, dims, jnp.float32) * scale * level
    return jnp.minimum(jnp.maximum(entries, -reach), reach).astype(kind)


def setup_inputs(seed: int = 0) -> dict:
    streams_of = jax.random.split(jax.random.key(seed), 8)
    return {
        "q_latent": draw_q_latent(jax.random.fold_in(streams_of[7], 71), 0),
        "q_gain": draw_q_gain(jax.random.fold_in(streams_of[7], 71), 0),
        "kv_cache": draw_kv_cache(jax.random.fold_in(streams_of[7], 71), 0),
        "kv_gain": draw_kv_gain(jax.random.fold_in(streams_of[7], 71), 0),
        "w_query": normal_values(streams_of[4], (QL, HEADS * (ND + RD)), QL ** -0.5, 0.15625, ((1, 2),)),
        "w_kv": normal_values(streams_of[5], (KL, HEADS * (ND + VD)), KL ** -0.5, 0.25, ((1, 2),)),
        "doc_lengths": ragged(streams_of[6], DOCS, SEQ, SEQ // 2, 0).astype(jnp.int32),
    }


epsilon = 1e-06

def rms_scale(rows, gain):
    values = rows.astype(jnp.float32)
    return values * lax.rsqrt(lax.optimization_barrier(jnp.mean(values * values, axis=-1, keepdims=True)) + epsilon) * gain

def doc_tables(doc_lengths, positions):
    doc_ends = jnp.cumsum(doc_lengths).astype(jnp.int32)
    passed = positions[:, None] >= doc_ends[None, :]
    doc_index = lax.optimization_barrier(jnp.sum(passed.astype(jnp.int32), axis=1)).astype(jnp.int32)
    doc_start = lax.optimization_barrier(jnp.sum(jnp.where(passed, doc_lengths[None, :], 0), axis=1)).astype(jnp.int32)
    return (doc_index, doc_start)

def rotate_pairs(values, offsets):
    half_width = values.shape[-1] // 2
    freq_index = jnp.arange(half_width, dtype=jnp.float32)
    frequency = jnp.exp(freq_index * (-2.0 * math.log(10000.0) / values.shape[-1]))
    angles = offsets.astype(jnp.float32)[:, None] * frequency[None, :]
    cosine = jnp.cos(angles)[:, None, :]
    sine_part = jnp.sin(angles)[:, None, :]
    lower_half = values[..., :half_width]
    upper_half = values[..., half_width:]
    return jnp.concatenate([lower_half * cosine - upper_half * sine_part, upper_half * cosine + lower_half * sine_part], axis=-1)

def project_queries(latent_rows, q_gain, w_query, offsets, nope_width, rope_width):
    normed = rms_scale(latent_rows, q_gain).astype(jnp.bfloat16)
    projected = jnp.dot(normed, w_query, preferred_element_type=jnp.float32)
    head_count = w_query.shape[1] // (nope_width + rope_width)
    projected = projected.reshape(latent_rows.shape[0], head_count, nope_width + rope_width)
    rotated = rotate_pairs(projected[..., nope_width:], offsets)
    return jnp.concatenate([projected[..., :nope_width], rotated], axis=-1).astype(jnp.bfloat16)

def reference(q_latent, q_gain, kv_cache, kv_gain, w_query, w_kv, doc_lengths):
    positions = jnp.arange(SEQ, dtype=jnp.int32)
    doc_index, doc_start = doc_tables(doc_lengths, positions)
    queries = project_queries(q_latent, q_gain, w_query, positions - doc_start, ND, RD)
    kv_normed = rms_scale(kv_cache[:, :KL], kv_gain).astype(jnp.bfloat16)
    expanded = jnp.dot(kv_normed, w_kv, preferred_element_type=jnp.float32).astype(jnp.bfloat16)
    expanded = expanded.reshape(SEQ, HEADS, ND + VD)
    key_rope = kv_cache[:, KL:]
    block_size = min(512, SEQ)
    window = min(SEQ, SEQ // 2 + block_size)
    score_scale = 1.0 / math.sqrt(ND + RD)

    def one_block(number):
        first_row = (number * block_size).astype(jnp.int32)
        key_first = jnp.clip(first_row + block_size - window, 0, SEQ - window).astype(jnp.int32)
        query_block = lax.dynamic_slice_in_dim(queries, first_row, block_size, 0).astype(jnp.float32)
        key_block = lax.dynamic_slice_in_dim(expanded, key_first, window, 0).astype(jnp.float32)
        rope_block = lax.dynamic_slice_in_dim(key_rope, key_first, window, 0).astype(jnp.float32)
        scores = jnp.einsum('qhd,khd->hqk', query_block[..., :ND], key_block[..., :ND])
        scores = (scores + jnp.einsum('qhr,kr->hqk', query_block[..., ND:], rope_block)) * score_scale
        query_pos = first_row + jnp.arange(block_size, dtype=jnp.int32)
        key_pos = key_first + jnp.arange(window, dtype=jnp.int32)
        query_doc = lax.dynamic_slice_in_dim(doc_index, first_row, block_size, 0)
        key_doc = lax.dynamic_slice_in_dim(doc_index, key_first, window, 0)
        allowed = (key_pos[None, :] <= query_pos[:, None]) & (key_doc[None, :] == query_doc[:, None])
        masked = jnp.where(allowed[None], scores, -1e+30)
        running_max = lax.optimization_barrier(jnp.max(masked, axis=-1))
        weights = jnp.where(allowed[None], jnp.exp(scores - running_max[..., None]), 0.0)
        row_total = lax.optimization_barrier(jnp.sum(weights, axis=-1))
        rounded = lax.optimization_barrier(weights.astype(jnp.bfloat16))
        mixed = jnp.einsum('hqk,khv->qhv', rounded.astype(jnp.float32), key_block[..., ND:])
        mixed = mixed / jnp.transpose(row_total)[:, :, None]
        return mixed.reshape(block_size, HEADS * VD)
    outputs = lax.map(one_block, jnp.arange(SEQ // block_size, dtype=jnp.int32))
    return outputs.reshape(SEQ, HEADS * VD).astype(jnp.bfloat16)
```

```python
import functools
import math

import jax
import jax.numpy as jnp
from jax import lax
from jax.experimental import pallas as pl
from jax.experimental.pallas import tpu as pltpu
from jax.sharding import PartitionSpec as P

KL = 512
RD = 64
ND = 128
VD = 128
LANES = 128
MESH = pl.DeviceIdType.MESH

epsilon = 1e-06


def normed(values, gain):
    values = values.astype(jnp.float32)
    mean = jnp.mean(values * values, axis=-1, keepdims=True)
    return (values * lax.rsqrt(mean + epsilon) * gain).astype(jnp.bfloat16)


def attend_kernel(
    nc, nh, step, len_ref, q_ref, qg_ref, kv_ref, kvg_ref, wq_hbm, wkv_hbm, out_ref,
    wq, wkv, q_own, kv_own, q_all, win, wk_t, kv_t, kr_even, kr_odd, query, key_t, value,
    bias, cos, sin, score_a, score_b, top_a, top_b,
    wq_sem, wkv_sem, q_send, q_recv, recv, y_send, z_send, x_send, c_send,
):
    c = lax.axis_index("ctx")
    h = lax.axis_index("head")
    rows, ql = q_ref.shape
    tok = rows * nh
    back = nc // 2
    keys = (back + 1) * tok
    heads = wkv.shape[1] // (ND + VD)
    docs = len_ref.shape[0]
    par = lax.rem(c, 2)
    col = lax.rem(lax.div(c, 2), 2)
    core = c + 1 - 2 * par
    side = c + 2 - 4 * col

    def wkv_copy():
        return pltpu.make_async_copy(wkv_hbm, wkv, wkv_sem)

    q_wide = step * (ND + RD)

    def wq_copy(i):
        at = pl.ds(i * q_wide, q_wide)
        return pltpu.make_async_copy(wq_hbm.at[:, at], wq.at[:, at], wq_sem.at[i])

    wkv_copy().start()
    for i in range(heads // step):
        wq_copy(i).start()

    barrier = pltpu.get_barrier_semaphore()

    def greet(ctx, head):
        pl.semaphore_signal(barrier, inc=1, device_id=(ctx, head), device_id_type=MESH)

    for k in range(1, nh):
        greet(c, lax.rem(h + k, nh))
    greet(core, h)
    greet(side, h)
    pl.when(c + 4 < nc)(lambda: greet(c + 4, h))
    pl.when(c >= 4)(lambda: greet(c - 4, h))

    kv_own[:, :KL] = normed(kv_ref[:, :KL], kvg_ref[...])
    kv_own[:, KL:] = kv_ref[:, KL:]
    q_own[...] = normed(q_ref[...], qg_ref[...])

    pl.semaphore_wait(barrier, nh + 1 + (c + 4 < nc).astype(jnp.int32) + (c >= 4).astype(jnp.int32))

    def part_rows(k):
        return pl.ds(pl.multiple_of(lax.rem(h - k + nh, nh) * rows, rows), rows)

    def part(d, k):
        return win.at[d, part_rows(k)]

    def remote(src, dst, send, got, ctx, head):
        return pltpu.make_async_remote_copy(
            src_ref=src, dst_ref=dst, send_sem=send, recv_sem=got, device_id=(ctx, head), device_id_type=MESH
        )

    def source(d, k):
        return kv_own if d == 0 and k == 0 else part(d, k)

    def y_copy(k):
        return remote(kv_own, part(0, 0), y_send.at[k], recv.at[0, k], c, lax.rem(h + k, nh))

    def q_copy(k):
        return remote(q_own, q_all.at[part_rows(0)], q_send.at[k], q_recv.at[k], c, lax.rem(h + k, nh))

    def z_copy(d, k):
        return remote(source(d, k), part(d + 4, k), z_send.at[d // 4, k], recv.at[d + 4, k], c + 4, h)

    def x_copy(d, to, k):
        return remote(source(d, k), part(to, k), x_send.at[d // 4, k], recv.at[to, k], side, h)

    def c_copy(d, to, k):
        return remote(source(d, k), part(to, k), c_send.at[d // 2, k], recv.at[to, k], core, h)

    def onward(d, k, act):
        here = c >= d
        if d % 4 == 0:
            if d + 4 <= back:
                pl.when(here & (c + 4 < nc))(lambda: act(z_copy(d, k)))
            if d + 2 <= back:
                pl.when(here & (col == 0))(lambda: act(x_copy(d, d + 2, k)))
            if d >= 2:
                pl.when(here & (col == 1))(lambda: act(x_copy(d, d - 2, k)))
        if d % 2 == 0:
            if d + 1 <= back:
                pl.when(here & (par == 0))(lambda: act(c_copy(d, d + 1, k)))
            if d >= 1:
                pl.when(here & (par == 1))(lambda: act(c_copy(d, d - 1, k)))

    def take(d, k):
        if d == 0:
            y_copy(k).wait_recv()
        else:
            pl.when(c >= d)(lambda: remote(part(d, k), part(d, k), recv.at[d, k], recv.at[d, k], c, h).wait_recv())
        onward(d, k, lambda copy: copy.start())

    for k in range(1, nh):
        y_copy(k).start()
    onward(0, 0, lambda copy: copy.start())
    for k in range(1, nh):
        q_copy(k).start()

    win[0, part_rows(0)] = kv_own[...]
    q_all[part_rows(0)] = q_own[...]
    for d in range(1, back + 1):
        @pl.when(c < d)
        def _(d=d):
            win[d] = jnp.zeros(win.shape[1:], win.dtype)

    first = c * tok

    def start_of(pos):
        start = jnp.zeros_like(pos)
        end = jnp.int32(0)
        for d in range(docs):
            end = end + len_ref[d]
            start = start + jnp.where(pos >= end, len_ref[d], 0)
        return start

    qpos = first + lax.broadcasted_iota(jnp.int32, (tok, tok), 0)
    kcol = first + lax.broadcasted_iota(jnp.int32, (tok, tok), 1)
    start = start_of(qpos)
    for d in range(back + 1):
        kpos = kcol - d * tok
        bias[:, d * tok : (d + 1) * tok] = jnp.where((kpos <= qpos) & (kpos >= start), 0.0, -1e30)
    pos = first + lax.broadcasted_iota(jnp.int32, (tok, LANES), 0)
    lane = lax.broadcasted_iota(jnp.int32, (tok, LANES), 1)
    turn_at = lax.rem(lane, RD)
    lower = turn_at < RD // 2
    freq_index = jnp.where(lower, turn_at, turn_at - RD // 2).astype(jnp.float32)
    frequency = jnp.exp(freq_index * (-2.0 * math.log(10000.0) / RD))
    angles = (pos - start_of(pos)).astype(jnp.float32) * frequency
    cos[...] = jnp.cos(angles)
    sine = jnp.sin(angles)
    sin[...] = jnp.where(lower, -sine, sine)

    wkv_copy().wait()

    def turn_weights(i, carry):
        for odd in range(2):
            n = 2 * i + odd
            at = pl.multiple_of(n * (ND + VD), ND + VD)
            flipped = wkv[:, pl.ds(at, ND)].T
            if odd:
                flipped = jnp.concatenate([flipped[ND // 2 :], flipped[: ND // 2]], axis=0)
            wk_t[pl.ds(pl.multiple_of(n * ND, ND), ND)] = flipped
        return carry

    lax.fori_loop(0, heads // 2, turn_weights, 0)

    def expand(slots):
        wide = len(slots) * tok
        for at, d in enumerate(slots):
            kv_t[:, at * tok : (at + 1) * tok] = win[d, :, :KL].T
            rope = win[d, :, KL:]
            blank = jnp.zeros((tok, LANES - RD), rope.dtype)
            kr_even[:, d * tok : (d + 1) * tok] = jnp.concatenate([rope, blank], axis=1).T
            kr_odd[:, d * tok : (d + 1) * tok] = jnp.concatenate([blank, rope], axis=1).T
        latent = win[slots[0], :, :KL]
        if len(slots) > 1:
            latent = jnp.concatenate([win[d, :, :KL] for d in slots], axis=0)

        def some(i, carry):
            rows_at = pl.ds(pl.multiple_of(i * step * ND, step * ND), step * ND)
            made = jnp.dot(wk_t[rows_at], kv_t[:, :wide], preferred_element_type=jnp.float32).astype(jnp.bfloat16)
            for at, d in enumerate(slots):
                key_t[rows_at, d * tok : (d + 1) * tok] = made[:, at * tok : (at + 1) * tok]
            for n in range(0, step, 2):
                at = pl.multiple_of((i * step + n) * (ND + VD), 2 * (ND + VD))
                pair = jnp.concatenate(
                    [wkv[:, pl.ds(at + ND, VD)], wkv[:, pl.ds(at + 2 * ND + VD, VD)]], axis=1
                )
                made = jnp.dot(latent, pair, preferred_element_type=jnp.float32).astype(jnp.bfloat16)
                to = pl.ds(pl.multiple_of((i * step + n) * VD, 2 * VD), 2 * VD)
                for s, d in enumerate(slots):
                    value[d * tok : (d + 1) * tok, to] = made[s * tok : (s + 1) * tok]
            return carry

        lax.fori_loop(0, heads // step, some, 0)

    def project():
        def some(i, carry):
            pltpu.make_async_copy(
                wq_hbm.at[:, pl.ds(0, q_wide)], wq.at[:, pl.ds(0, q_wide)], wq_sem.at[i]
            ).wait()
            at = pl.multiple_of(i * q_wide, q_wide)
            for n in range(0, step, 2):
                off = n * (ND + RD)
                made = jnp.dot(
                    q_all[...], wq[:, pl.ds(at + off, 2 * (ND + RD))], preferred_element_type=jnp.float32
                )
                one, two, three = (made[:, j * LANES : (j + 1) * LANES] for j in range(3))
                low = lane < LANES // 2
                rope = jnp.where(low, two, three)
                other = jnp.where(lower, pltpu.roll(rope, LANES - RD // 2, 1), pltpu.roll(rope, RD // 2, 1))
                rope = rope * cos[...] + other * sin[...]
                both = jnp.concatenate([one, jnp.where(low, three, two), rope], axis=1)
                query[:, pl.ds(at + off, 2 * (ND + RD))] = both.astype(jnp.bfloat16)
            return carry

        lax.fori_loop(0, heads // step, some, 0)

    order = [0] + [d for d in range(4, back + 1, 4)] + [d for d in range(2, back + 1, 4)] + [d for d in range(1, back + 1, 2)]
    for k in range(1, nh):
        take(0, k)
    for d in range(4, back + 1, 4):
        for k in range(nh):
            take(d, k)
        if d == 4:
            expand([0, 4])
    for d in range(2, back + 1, 4):
        for k in range(nh):
            take(d, k)
    for k in range(1, nh):
        q_copy(k).wait_recv()
    project()
    for d in range(1, back + 1, 2):
        for k in range(nh):
            take(d, k)
    rest = [d for d in order if d not in (0, 4)]
    for at in range(0, len(rest), 2):
        expand(rest[at : at + 2])

    scale = math.log2(math.e) / math.sqrt(ND + RD)

    def score(m, odd, to, top):
        base = pl.multiple_of(m * 2 * (ND + RD), 2 * (ND + RD))
        left = jnp.concatenate(
            [query[:, pl.ds(base + odd * ND, ND)], query[:, pl.ds(base + 2 * ND, 2 * RD)]], axis=1
        )
        turned = kr_odd if odd else kr_even
        right = jnp.concatenate([key_t[pl.ds(pl.multiple_of((2 * m + odd) * ND, ND), ND)], turned[...]], axis=0)
        made = jnp.dot(left, right, preferred_element_type=jnp.float32) + bias[...]
        to[...] = made
        top[...] = jnp.max(made, axis=1, keepdims=True)

    def mix(n, made, top):
        weights = jnp.exp2((made[...] - top[...]) * scale)
        total = jnp.sum(weights, axis=1, keepdims=True)
        at = pl.ds(pl.multiple_of(n * VD, VD), VD)
        mixed = jnp.dot(weights.astype(jnp.bfloat16), value[:, at], preferred_element_type=jnp.float32)
        out_ref[:, at] = (mixed / total).astype(jnp.bfloat16)

    score(0, 0, score_a, top_a)

    def pair(m, carry):
        score(m, 1, score_b, top_b)
        mix(2 * m, score_a, top_a)
        score(jnp.minimum(m + 1, heads // 2 - 1), 0, score_a, top_a)
        mix(2 * m + 1, score_b, top_b)
        return carry

    lax.fori_loop(0, heads // 2, pair, 0)

    for k in range(1, nh):
        y_copy(k).wait_send()
        q_copy(k).wait_send()
    for d in range(0, back + 1, 2):
        for k in range(nh):
            onward(d, k, lambda copy: copy.wait_send())


def attend(doc_lengths, q_latent, q_gain, kv_cache, kv_gain, w_query, w_kv, nc, nh):
    rows, ql = q_latent.shape
    width = kv_cache.shape[1]
    tok = rows * nh
    back = nc // 2
    keys = (back + 1) * tok
    heads = w_kv.shape[1] // (ND + VD)
    step = min(8, heads)
    bf16, f32 = jnp.bfloat16, jnp.float32
    dma = pltpu.SemaphoreType.DMA
    vmem = pl.BlockSpec(memory_space=pltpu.VMEM)
    hbm = pl.BlockSpec(memory_space=pl.ANY)
    smem = pl.BlockSpec(memory_space=pltpu.SMEM)
    return pl.pallas_call(
        functools.partial(attend_kernel, nc, nh, step),
        out_shape=jax.ShapeDtypeStruct((tok, heads * VD), bf16),
        in_specs=[smem, vmem, vmem, vmem, vmem, hbm, hbm],
        out_specs=vmem,
        scratch_shapes=[
            pltpu.VMEM(w_query.shape, bf16),
            pltpu.VMEM(w_kv.shape, bf16),
            pltpu.VMEM((rows, ql), bf16),
            pltpu.VMEM((rows, width), bf16),
            pltpu.VMEM((tok, ql), bf16),
            pltpu.VMEM((back + 1, tok, width), bf16),
            pltpu.VMEM((heads * ND, KL), bf16),
            pltpu.VMEM((KL, 2 * tok), bf16),
            pltpu.VMEM((LANES, keys), bf16),
            pltpu.VMEM((LANES, keys), bf16),
            pltpu.VMEM((tok, heads * (ND + RD)), bf16),
            pltpu.VMEM((heads * ND, keys), bf16),
            pltpu.VMEM((keys, heads * VD), bf16),
            pltpu.VMEM((tok, keys), f32),
            pltpu.VMEM((tok, LANES), f32),
            pltpu.VMEM((tok, LANES), f32),
            pltpu.VMEM((tok, keys), f32),
            pltpu.VMEM((tok, keys), f32),
            pltpu.VMEM((tok, 1), f32),
            pltpu.VMEM((tok, 1), f32),
            dma((heads // step,)), dma, dma((nh,)), dma((nh,)), dma((back + 1, nh)), dma((nh,)),
            dma((back // 4 + 1, nh)), dma((back // 4 + 1, nh)), dma((back // 2 + 1, nh)),
        ],
        compiler_params=pltpu.CompilerParams(
            collective_id=0, has_side_effects=True, vmem_limit_bytes=67043328
        ),
        name="attend",
    )(doc_lengths, q_latent, q_gain, kv_cache, kv_gain, w_query, w_kv)


def solution(mesh):
    nc, nh = mesh.shape["ctx"], mesh.shape["head"]

    def body(q_latent, q_gain, kv_cache, kv_gain, w_query, w_kv, doc_lengths):
        return attend(doc_lengths, q_latent, q_gain[None], kv_cache, kv_gain[None], w_query, w_kv, nc, nh)

    placed = (
        P(("ctx", "head"), None),
        P(),
        P(("ctx", "head"), None),
        P(),
        P(None, "head"),
        P(None, "head"),
        P(),
    )
    return jax.shard_map(body, mesh=mesh, in_specs=placed, out_specs=P("ctx", "head"), check_vma=False)
```

```python
import functools
import math

import jax
import jax.numpy as jnp
from jax import lax
from jax.experimental import pallas as pl
from jax.experimental.pallas import tpu as pltpu
from jax.sharding import PartitionSpec as P

KL = 512
RD = 64
ND = 128
VD = 128
LANES = 128
MESH = pl.DeviceIdType.MESH

epsilon = 1e-06


def normed(values, gain):
    values = values.astype(jnp.float32)
    mean = jnp.mean(values * values, axis=-1, keepdims=True)
    return (values * lax.rsqrt(mean + epsilon) * gain).astype(jnp.bfloat16)


def attend_kernel(
    nc, nh, step, len_ref, q_ref, qg_ref, kv_ref, kvg_ref, wq_hbm, wkv_hbm, out_ref,
    wq, wkv, q_own, kv_own, q_all, win, wk_t, kv_t, rope_t, query, key_t, value,
    bias, cos, sin, scores, tops,
    wq_sem, wkv_sem, q_send, q_recv, recv, y_send, z_send, x_send,
    key_send, key_recv, value_send, value_recv, rope_send, rope_recv,
):
    c = lax.axis_index("ctx")
    h = lax.axis_index("head")
    rows, ql = q_ref.shape
    tok = rows * nh
    back = nc // 2
    heads = wkv.shape[1] // (ND + VD)
    turns = heads // step
    docs = len_ref.shape[0]
    par = lax.rem(c, 2)
    col = lax.rem(lax.div(c, 2), 2)
    core = c + 1 - 2 * par
    side = c + 2 - 4 * col

    def wkv_copy():
        return pltpu.make_async_copy(wkv_hbm, wkv, wkv_sem)

    q_wide = step * (ND + RD)

    def wq_copy(i):
        at = pl.ds(i * q_wide, q_wide)
        return pltpu.make_async_copy(wq_hbm.at[:, at], wq.at[:, at], wq_sem.at[i])

    wkv_copy().start()

    barrier = pltpu.get_barrier_semaphore()

    def greet(ctx, head):
        pl.semaphore_signal(barrier, inc=1, device_id=(ctx, head), device_id_type=MESH)

    for k in range(1, nh):
        greet(c, lax.rem(h + k, nh))
    greet(core, h)
    greet(side, h)
    pl.when(c + 4 < nc)(lambda: greet(c + 4, h))
    pl.when(c >= 4)(lambda: greet(c - 4, h))

    kv_own[:, :KL] = normed(kv_ref[:, :KL], kvg_ref[...])
    kv_own[:, KL:] = kv_ref[:, KL:]
    q_own[...] = normed(q_ref[...], qg_ref[...])

    first = c * tok

    def start_of(pos):
        start = jnp.zeros_like(pos)
        end = jnp.int32(0)
        for d in range(docs):
            end = end + len_ref[d]
            start = start + jnp.where(pos >= end, len_ref[d], 0)
        return start

    qpos = first + lax.broadcasted_iota(jnp.int32, (tok, tok), 0)
    kcol = first + lax.broadcasted_iota(jnp.int32, (tok, tok), 1)
    start = start_of(qpos)
    for d in range(back + 1):
        kpos = kcol - d * tok
        bias[:, d * tok : (d + 1) * tok] = jnp.where((kpos <= qpos) & (kpos >= start), 0.0, -1e30)
    pos = first + lax.broadcasted_iota(jnp.int32, (tok, LANES), 0)
    lane = lax.broadcasted_iota(jnp.int32, (tok, LANES), 1)
    turn_at = lax.rem(lane, RD)
    lower = turn_at < RD // 2
    freq_index = jnp.where(lower, turn_at, turn_at - RD // 2).astype(jnp.float32)
    frequency = jnp.exp(freq_index * (-2.0 * math.log(10000.0) / RD))
    angles = (pos - start_of(pos)).astype(jnp.float32) * frequency
    cos[...] = jnp.cos(angles)
    sine = jnp.sin(angles)
    sin[...] = jnp.where(lower, -sine, sine)

    wkv_copy().wait()
    for i in range(turns):
        wq_copy(i).start()

    def turn_weights(i, carry):
        for odd in range(2):
            n = 2 * i + odd
            at = pl.multiple_of(n * (ND + VD), ND + VD)
            flipped = wkv[:, pl.ds(at, ND)].T
            if odd:
                flipped = jnp.concatenate([flipped[ND // 2 :], flipped[: ND // 2]], axis=0)
            wk_t[pl.ds(pl.multiple_of(n * ND, ND), ND)] = flipped
        return carry

    lax.fori_loop(0, heads // 4, turn_weights, 0)

    pl.semaphore_wait(barrier, nh + 1 + (c + 4 < nc).astype(jnp.int32) + (c >= 4).astype(jnp.int32))

    def part_rows(k):
        return pl.ds(pl.multiple_of(lax.rem(h - k + nh, nh) * rows, rows), rows)

    def part(d, k):
        return win.at[d // 2, part_rows(k)]

    def remote(src, dst, send, got, ctx, head):
        return pltpu.make_async_remote_copy(
            src_ref=src, dst_ref=dst, send_sem=send, recv_sem=got, device_id=(ctx, head), device_id_type=MESH
        )

    def source(d, k):
        return kv_own if d == 0 and k == 0 else part(d, k)

    def y_copy(k):
        return remote(kv_own, part(0, 0), y_send.at[k], recv.at[0, k], c, lax.rem(h + k, nh))

    def q_copy(k):
        return remote(q_own, q_all.at[part_rows(0)], q_send.at[k], q_recv.at[k], c, lax.rem(h + k, nh))

    def z_copy(d, k):
        return remote(source(d, k), part(d + 4, k), z_send.at[d // 4, k], recv.at[d // 2 + 2, k], c + 4, h)

    def x_copy(d, to, k):
        return remote(source(d, k), part(to, k), x_send.at[d // 4, k], recv.at[to // 2, k], side, h)

    def onward(d, k, act):
        here = c >= d
        if d % 4 == 0:
            if d + 4 <= back:
                pl.when(here & (c + 4 < nc))(lambda: act(z_copy(d, k)))
            if d + 2 <= back:
                pl.when(here & (col == 0))(lambda: act(x_copy(d, d + 2, k)))
            if d >= 2:
                pl.when(here & (col == 1))(lambda: act(x_copy(d, d - 2, k)))

    def take(d, k):
        if d == 0:
            y_copy(k).wait_recv()
        else:
            pl.when(c >= d)(lambda: remote(part(d, k), part(d, k), recv.at[d // 2, k], recv.at[d // 2, k], c, h).wait_recv())
        onward(d, k, lambda copy: copy.start())

    for k in range(1, nh):
        y_copy(k).start()
    onward(0, 0, lambda copy: copy.start())
    for k in range(1, nh):
        q_copy(k).start()

    win[0, part_rows(0)] = kv_own[...]
    q_all[part_rows(0)] = q_own[...]
    for d in range(2, back + 1, 2):
        @pl.when(c < d)
        def _(d=d):
            win[d // 2] = jnp.zeros(win.shape[1:], win.dtype)

    lax.fori_loop(heads // 4, heads // 2, turn_weights, 0)

    def shared(d, act):
        if d == 0:
            pl.when(par == 0)(act)
        elif d == back:
            pl.when(par == 1)(act)
        else:
            act()

    def key_rows(i):
        return pl.ds(pl.multiple_of(i * step * ND, step * ND), step * ND)

    def value_cols(i):
        return pl.ds(pl.multiple_of(i * step * VD, step * VD), step * VD)

    def copies(d, i):
        to = d + 1 - 2 * par
        at = lax.div(to, 2)
        return (
            remote(key_t.at[d, key_rows(i)], key_t.at[to, key_rows(i)], key_send.at[d // 2, i], key_recv.at[at, i], core, h),
            remote(
                value.at[d, :, value_cols(i)], value.at[to, :, value_cols(i)],
                value_send.at[d // 2, i], value_recv.at[at, i], core, h,
            ),
        )

    def rope_copy(d):
        to = d + 1 - 2 * par
        return remote(rope_t.at[d], rope_t.at[to], rope_send.at[d // 2], rope_recv.at[lax.div(to, 2)], core, h)

    def share(d, i):
        def act():
            for copy in copies(d, i):
                copy.start()

        shared(d, act)

    def expand(slots):
        wide = len(slots) * tok
        for at, d in enumerate(slots):
            kv_t[:, at * tok : (at + 1) * tok] = win[d // 2, :, :KL].T
            rope = win[d // 2, :, KL:]
            rope_t[d] = jnp.concatenate([rope, jnp.zeros((tok, LANES - RD), rope.dtype)], axis=1).T

        def some(i):
            made = jnp.dot(wk_t[key_rows(i)], kv_t[:, :wide], preferred_element_type=jnp.float32).astype(jnp.bfloat16)
            for at, d in enumerate(slots):
                key_t[d, key_rows(i)] = made[:, at * tok : (at + 1) * tok]
            latent = [win[d // 2, :, :KL] for d in slots]
            latent = jnp.concatenate(latent, axis=0) if len(slots) > 1 else latent[0]
            for n in range(0, step, 2):
                at = pl.multiple_of((i * step + n) * (ND + VD), 2 * (ND + VD))
                pair = jnp.concatenate(
                    [wkv[:, pl.ds(at + ND, VD)], wkv[:, pl.ds(at + 2 * ND + VD, VD)]], axis=1
                )
                made = jnp.dot(latent, pair, preferred_element_type=jnp.float32).astype(jnp.bfloat16)
                to = pl.ds(pl.multiple_of((i * step + n) * VD, 2 * VD), 2 * VD)
                for at, d in enumerate(slots):
                    value[d, :, to] = made[at * tok : (at + 1) * tok]

        def later(i, carry):
            some(i)
            for d in slots:
                share(d, i - 1)
            return carry

        some(0)
        for d in slots:
            shared(d, lambda d=d: rope_copy(d).start())
        lax.fori_loop(1, turns, later, 0)
        return lambda: [share(d, turns - 1) for d in slots]

    def project(begin, end):
        def some(i, carry):
            pltpu.make_async_copy(
                wq_hbm.at[:, pl.ds(0, q_wide)], wq.at[:, pl.ds(0, q_wide)], wq_sem.at[i]
            ).wait()
            at = pl.multiple_of(i * q_wide, q_wide)
            for n in range(0, step, 2):
                off = n * (ND + RD)
                made = jnp.dot(
                    q_all[...], wq[:, pl.ds(at + off, 2 * (ND + RD))], preferred_element_type=jnp.float32
                )
                one, two, three = (made[:, j * LANES : (j + 1) * LANES] for j in range(3))
                low = lane < LANES // 2
                rope = jnp.where(low, two, three)
                other = jnp.where(lower, pltpu.roll(rope, LANES - RD // 2, 1), pltpu.roll(rope, RD // 2, 1))
                rope = rope * cos[...] + other * sin[...]
                both = jnp.concatenate([one, jnp.where(low, three, two), rope], axis=1)
                query[:, pl.ds(at + off, 2 * (ND + RD))] = both.astype(jnp.bfloat16)
            return carry

        lax.fori_loop(begin, end, some, 0)

    column = list(range(0, back + 1, 4))
    beside = list(range(2, back + 1, 4))
    for k in range(1, nh):
        take(0, k)
    for k in range(nh):
        take(4, k)
    early = 8 <= back
    if early:
        take(8, 0)
    last = expand([0, 4])
    for d in column[2:]:
        for k in range(1 if early and d == 8 else 0, nh):
            take(d, k)
    for k in range(1, nh):
        q_copy(k).wait_recv()
    last()
    project(0, turns // 2)
    rest = beside[:1] + column[2:] + beside[1:]
    for at in range(0, len(rest), 2):
        slots = rest[at : at + 2]
        for d in slots:
            if d in beside:
                for k in range(nh):
                    take(d, k)
        if at:
            last()
        last = expand(slots)
    project(turns // 2, turns - 1)
    last()
    project(turns - 1, turns)

    def arrived(i):
        for d in range(0, back, 2):
            for ref, sem in ((key_t.at[d + 1, key_rows(i)], key_recv), (value.at[d + 1, :, value_cols(i)], value_recv)):
                remote(ref, ref, sem.at[d // 2, i], sem.at[d // 2, i], core, h).wait_recv()

    for d in range(0, back, 2):
        ref = rope_t.at[d + 1]
        remote(ref, ref, rope_recv.at[d // 2], rope_recv.at[d // 2], core, h).wait_recv()
    arrived(0)

    scale = math.log2(math.e) / math.sqrt(ND + RD)

    slots = range(back + 1)

    def score(m, at):
        base = pl.multiple_of(m * 2 * (ND + RD), 2 * (ND + RD))
        for odd in range(2):
            left = jnp.concatenate(
                [query[:, pl.ds(base + odd * ND, ND)], query[:, pl.ds(base + 2 * ND, 2 * RD)]], axis=1
            )
            rows_at = pl.ds(pl.multiple_of((2 * m + odd) * ND, ND), ND)
            plain = jnp.concatenate([key_t[d, rows_at] for d in slots], axis=1)
            rope = jnp.concatenate([rope_t[d] for d in slots], axis=1)
            parts = [plain, rope[RD:], rope[:RD]] if odd else [plain, rope]
            made = jnp.dot(left, jnp.concatenate(parts, axis=0), preferred_element_type=jnp.float32) + bias[...]
            scores[2 * at + odd][...] = made
            tops[2 * at + odd][...] = jnp.max(made, axis=1, keepdims=True)

    def mix(m, at):
        for odd in range(2):
            weights = jnp.exp2((scores[2 * at + odd][...] - tops[2 * at + odd][...]) * scale)
            total = jnp.sum(weights, axis=1, keepdims=True)
            cols = pl.ds(pl.multiple_of((2 * m + odd) * VD, VD), VD)
            values = jnp.concatenate([value[d, :, cols] for d in slots], axis=0)
            mixed = jnp.dot(weights.astype(jnp.bfloat16), values, preferred_element_type=jnp.float32)
            out_ref[:, cols] = (mixed / total).astype(jnp.bfloat16)

    score(0, 0)
    per = step // 4

    def four(t, carry):
        @pl.when((lax.rem(t + 1, per) == 0) & (t + 1 < heads // 4))
        def _():
            arrived(lax.div(t + 1, per))

        score(2 * t + 1, 1)
        mix(2 * t, 0)
        score(jnp.minimum(2 * t + 2, heads // 2 - 1), 0)
        mix(2 * t + 1, 1)
        return carry

    lax.fori_loop(0, heads // 4, four, 0)

    for k in range(1, nh):
        y_copy(k).wait_send()
        q_copy(k).wait_send()
    for d in range(0, back + 1, 2):
        for k in range(nh):
            onward(d, k, lambda copy: copy.wait_send())

        def sent(d=d):
            rope_copy(d).wait_send()
            for i in range(turns):
                for copy in copies(d, i):
                    copy.wait_send()

        shared(d, sent)


def attend(doc_lengths, q_latent, q_gain, kv_cache, kv_gain, w_query, w_kv, nc, nh):
    rows, ql = q_latent.shape
    width = kv_cache.shape[1]
    tok = rows * nh
    back = nc // 2
    keys = (back + 1) * tok
    heads = w_kv.shape[1] // (ND + VD)
    step = min(8, heads)
    turns = heads // step
    even = back // 2 + 1
    bf16, f32 = jnp.bfloat16, jnp.float32
    dma = pltpu.SemaphoreType.DMA
    vmem = pl.BlockSpec(memory_space=pltpu.VMEM)
    hbm = pl.BlockSpec(memory_space=pl.ANY)
    smem = pl.BlockSpec(memory_space=pltpu.SMEM)
    return pl.pallas_call(
        functools.partial(attend_kernel, nc, nh, step),
        out_shape=jax.ShapeDtypeStruct((tok, heads * VD), bf16),
        in_specs=[smem, vmem, vmem, vmem, vmem, hbm, hbm],
        out_specs=vmem,
        scratch_shapes=[
            pltpu.VMEM(w_query.shape, bf16),
            pltpu.VMEM(w_kv.shape, bf16),
            pltpu.VMEM((rows, ql), bf16),
            pltpu.VMEM((rows, width), bf16),
            pltpu.VMEM((tok, ql), bf16),
            pltpu.VMEM((even, tok, width), bf16),
            pltpu.VMEM((heads * ND, KL), bf16),
            pltpu.VMEM((KL, 2 * tok), bf16),
            pltpu.VMEM((back + 1, LANES, tok), bf16),
            pltpu.VMEM((tok, heads * (ND + RD)), bf16),
            pltpu.VMEM((back + 1, heads * ND, tok), bf16),
            pltpu.VMEM((back + 1, tok, heads * VD), bf16),
            pltpu.VMEM((tok, keys), f32),
            pltpu.VMEM((tok, LANES), f32),
            pltpu.VMEM((tok, LANES), f32),
            [pltpu.VMEM((tok, keys), f32)] * 4,
            [pltpu.VMEM((tok, 1), f32)] * 4,
            dma((turns,)), dma, dma((nh,)), dma((nh,)), dma((even, nh)), dma((nh,)), dma((even, nh)), dma((even, nh)),
            dma((even, turns)), dma((even, turns)), dma((even, turns)), dma((even, turns)), dma((even,)), dma((even,)),
        ],
        compiler_params=pltpu.CompilerParams(
            collective_id=0, has_side_effects=True, vmem_limit_bytes=67043328
        ),
        name="attend",
    )(doc_lengths, q_latent, q_gain, kv_cache, kv_gain, w_query, w_kv)


def solution(mesh):
    nc, nh = mesh.shape["ctx"], mesh.shape["head"]

    def body(q_latent, q_gain, kv_cache, kv_gain, w_query, w_kv, doc_lengths):
        return attend(doc_lengths, q_latent, q_gain[None], kv_cache, kv_gain[None], w_query, w_kv, nc, nh)

    placed = (
        P(("ctx", "head"), None),
        P(),
        P(("ctx", "head"), None),
        P(),
        P(None, "head"),
        P(None, "head"),
        P(),
    )
    return jax.shard_map(body, mesh=mesh, in_specs=placed, out_specs=P("ctx", "head"), check_vma=False)
```
